32 devices in a mesh: walker: 4 (over y, x), vec: 8 (over z, core).
Axes of the slice: x: 2, y: 2, z: 4, core: 2. Of those that a mesh axis runs over, the one named last changes fastest.
Arguments:
- walkers: bfloat16 [128, 128, 1024], P(('walker', 'vec')), may hold values from -6 to 6
- propagator: bfloat16 [1024, 1024], replicated, may hold values from -0.1875 to 0.1875
- chol: bfloat16 [64, 128, 1024], P('vec'), may hold values from -0.1875 to 0.1875
- parent_group: int32 [4, 8, 4], P(None, 'vec'), may hold values from 0 to 3, as said below
- parent_slot: int32 [4, 8, 4], P(None, 'vec'), may hold values from 0 to 3
- live_count: int32 [4, 8], P('walker', 'vec'), may hold values from 1 to 4, as said below
Outputs:
- new_walkers: bfloat16 [128, 128, 1024], P(('walker', 'vec'))
- energy: float32 [4, 8, 4], P('walker', 'vec')
The draws below stay inside these ranges and needn't reach their ends.
Inputs may be any that keep to these rules, and one draw needn't show every extreme that they name: For each d and b the 4 entries parent_group[d, b, :] are different groups. `live_count`: some device has all 4 slots live.
All inputs are finite; a program needn't handle non-finite values.
Results may differ from the reference program's by a relative error of at most 0.0047.
Values may be sent and summed in bfloat16 or wider, within the bound.
No kernel may reach another device: no remote copies, remote signals or barrier semaphores. Data moves between devices by JAX's collectives and lax.ppermute only.
A program may use at most 192 MiB of HBM per device.

```python
import jax
import jax.numpy as jnp
from jax import lax

NEL = 128
NORB = 1024
W_DEV = 4
NCHOL = 64
NW_TOT = 128
N_WALKER = 4
N_VEC = 8


def draw_parent_group(key, part):
    keys = jax.random.split(jax.random.fold_in(key, 11), N_WALKER * N_VEC)
    perms = jax.vmap(lambda one: jax.random.permutation(one, N_WALKER))(keys)
    return perms[:, :W_DEV].reshape(N_WALKER, N_VEC, W_DEV).astype(jnp.int32)


def draw_live_count(key, part):
    counts = jax.random.randint(jax.random.fold_in(key, 23), (N_WALKER, N_VEC), 1, W_DEV + 1)
    return counts.at[0, 0].set(W_DEV).astype(jnp.int32)


def set_ends(drawn, stream_key, least, top_value):
    longest = drawn.shape.index(max(drawn.shape))
    spots = []
    for shift in (0, 1):
        where = [jax.random.randint(jax.random.fold_in(stream_key, axis), (), 0, length) for axis, length in enumerate(drawn.shape)]
        where[longest] = (where[longest] + shift) % drawn.shape[longest]
        spots.append(tuple(where))
    return drawn.at[spots[0]].set(least).at[spots[1]].set(top_value)


def levels(rng, dims, cuts, least, high):
    loudness = 1.0
    for dim, parts in cuts:
        draws = jax.random.uniform(jax.random.fold_in(jax.random.fold_in(rng, 6), dim), (parts,), jnp.float32, least / len(cuts), high / len(cuts))
        loudness = loudness * jnp.repeat(jnp.exp(draws), dims[dim] // parts).reshape((-1,) + (1,) * (len(dims) - 1 - dim))
    return loudness


def bell_draw(rng, extent, scale, bound, cuts=(), kind=jnp.bfloat16):
    loudness = levels(rng, extent, cuts, -0.22, 0.18) if cuts else 1.0
    drawn = jax.random.normal(rng, extent, jnp.float32) * scale * loudness
    return jnp.minimum(jnp.maximum(drawn, -bound), bound).astype(kind)


def setup_inputs(seed: int = 0) -> dict:
    seeds = jax.random.split(jax.random.key(seed), 7)
    return {
        "walkers": bell_draw(seeds[0], (NW_TOT, NEL, NORB), 1.0, 6.0, ((0, 32),)),
        "propagator": bell_draw(seeds[1], (NORB, NORB), NORB ** -0.5, 0.1875),
        "chol": bell_draw(seeds[2], (NCHOL, NEL, NORB), NORB ** -0.5, 0.1875, ((0, 8),)),
        "parent_group": draw_parent_group(jax.random.fold_in(seeds[6], 71), 0),
        "parent_slot": set_ends(jax.random.randint(seeds[4], (N_WALKER, N_VEC, W_DEV), 0, W_DEV), jax.random.fold_in(seeds[4], 1), 0, W_DEV - 1).astype(jnp.int32),
        "live_count": draw_live_count(jax.random.fold_in(seeds[6], 71), 0),
    }


def walker_energy(single, flat_chol):
    prod = jnp.dot(flat_chol, single.astype(jnp.float32).T).reshape(NCHOL, NEL, NEL)
    trace = jnp.trace(prod, axis1=1, axis2=2)
    cross = jnp.einsum('gij,gji->', prod, prod)
    return 0.5 * (jnp.sum(trace * trace) - cross) / (NCHOL * NEL)


def reference(walkers, propagator, chol, parent_group, parent_slot, live_count):
    moved = jnp.dot(walkers.reshape(-1, NORB), propagator, preferred_element_type=jnp.float32)
    moved = moved.astype(jnp.bfloat16).reshape(N_WALKER, N_VEC, W_DEV, NEL, NORB)
    column = jnp.arange(N_VEC, dtype=jnp.int32)[None, :, None]
    picked = moved[parent_group, column, parent_slot]
    keep = jnp.arange(W_DEV, dtype=jnp.int32)[None, None, :] < live_count[:, :, None]
    fresh = jnp.where(keep[..., None, None], picked, jnp.zeros_like(picked))
    flat_new = fresh.reshape(NW_TOT, NEL, NORB)
    flat_chol = chol.reshape(NCHOL * NEL, NORB).astype(jnp.float32)
    energy = lax.map(lambda single: walker_energy(single, flat_chol), flat_new)
    return flat_new, energy.reshape(N_WALKER, N_VEC, W_DEV)
```

```python
import functools

import jax
import jax.numpy as jnp
from jax import lax
from jax.experimental import pallas as pl
from jax.experimental.pallas import tpu as pltpu
from jax.sharding import PartitionSpec as P

CORES = 2
VMEM_BYTES = 48 * 1024 * 1024


def swap(value, axis, mask):
    size = lax.axis_size(axis)
    return lax.ppermute(value, axis, [(i, i ^ mask) for i in range(size)])


def pair_terms(vectors, blocks, rows, eye):
    nel = eye.shape[0]
    count_v, count_b = vectors.shape[0] // nel, blocks.shape[0] // nel
    t = lax.dot_general(vectors, blocks, (((1,), (1,)), ((), ())), preferred_element_type=jnp.float32)
    crosses, diagonals = [], []
    for b in range(count_b):
        cross, diags = None, []
        for v in range(count_v):
            tile = t[v * nel : (v + 1) * nel, b * nel : (b + 1) * nel]
            both = jnp.sum((tile * tile.T).reshape(nel // rows, rows, nel), axis=0)
            cross = both if cross is None else cross + both
            diags.append(jnp.sum(jnp.where(eye, tile, 0.0), axis=0, keepdims=True))
        crosses.append(cross)
        diagonals.append(diags)
    return crosses, diagonals


def energy_kernel(n_blocks, n_vectors, *refs):
    block_refs, vector_refs, out_ref = refs[:n_blocks], refs[n_blocks : n_blocks + n_vectors], refs[-1]
    nel, norb = block_refs[0].shape[1:]
    eye = lax.broadcasted_iota(jnp.int32, (nel, nel), 0) == lax.broadcasted_iota(jnp.int32, (nel, nel), 1)
    row = 0
    for block_ref in block_refs:
        count = block_ref.shape[0]
        group = 4 if count % 4 == 0 else 2 if count % 2 == 0 else 1

        def step(i, carry, block_ref=block_ref, group=group, row=row):
            blocks = block_ref[pl.ds(i * group, group)].reshape(group * nel, norb)
            crosses, diagonals = [None] * group, [[] for _ in range(group)]
            for vector_ref in vector_refs:
                total = vector_ref.shape[0]
                wide = 2 if total % 2 == 0 else 1
                for v in range(0, total, wide):
                    vectors = vector_ref[v : v + wide].reshape(wide * nel, norb)
                    cross, diags = pair_terms(vectors, blocks, 8, eye)
                    for b in range(group):
                        crosses[b] = cross[b] if crosses[b] is None else crosses[b] + cross[b]
                        diagonals[b] += diags[b]
            for b in range(group):
                trace = jnp.sum(jnp.concatenate(diagonals[b], axis=0), axis=1, keepdims=True)
                cross = jnp.sum(jnp.sum(crosses[b], axis=1, keepdims=True), axis=0, keepdims=True)
                value = jnp.sum(trace * trace, axis=0, keepdims=True) - cross
                out_ref[pl.ds(row + i * group + b, 1), :] = jnp.broadcast_to(value, (1, nel))
            return carry

        lax.fori_loop(0, count // group, step, 0)
        row += count


def energy_terms(blocks, vectors):
    nel, norb = blocks[0].shape[1:]
    total_b, total_v = sum(b.shape[0] for b in blocks), sum(v.shape[0] for v in vectors)
    return pl.pallas_call(
        functools.partial(energy_kernel, len(blocks), len(vectors)),
        out_shape=jax.ShapeDtypeStruct((total_b, nel), jnp.float32),
        in_specs=[pl.BlockSpec(memory_space=pltpu.VMEM)] * (len(blocks) + len(vectors)),
        out_specs=pl.BlockSpec(memory_space=pltpu.VMEM),
        compiler_params=pltpu.CompilerParams(vmem_limit_bytes=VMEM_BYTES),
        cost_estimate=pl.CostEstimate(
            flops=2 * total_b * total_v * nel * nel * norb,
            bytes_accessed=2 * (total_b + total_v) * nel * norb,
            transcendentals=0,
        ),
        name="energy_terms",
    )(*blocks, *vectors)


def select_kernel(sizes, which_ref, slot_ref, keep_ref, *refs):
    sources, out_ref, sem = refs[: len(sizes)], refs[-2], refs[-1]
    k = pl.program_id(0)

    @pl.when(keep_ref[k] == 0)
    def _():
        out_ref[...] = jnp.zeros_like(out_ref)

    for i, source in enumerate(sources):

        @pl.when((keep_ref[k] != 0) & (which_ref[k] == i))
        def _(source=source):
            copy = pltpu.make_async_copy(source.at[pl.ds(slot_ref[k], 1)], out_ref, sem)
            copy.start()
            copy.wait()


def select(sources, which, slot, keep):
    nel, norb = sources[0].shape[1:]
    count = which.shape[0]
    return pl.pallas_call(
        functools.partial(select_kernel, [s.shape[0] for s in sources]),
        out_shape=jax.ShapeDtypeStruct((count, nel, norb), sources[0].dtype),
        grid_spec=pltpu.PrefetchScalarGridSpec(
            num_scalar_prefetch=3,
            grid=(count,),
            in_specs=[pl.BlockSpec(memory_space=pl.ANY)] * len(sources),
            out_specs=pl.BlockSpec((1, nel, norb), lambda k, *_: (k, 0, 0)),
            scratch_shapes=[pltpu.SemaphoreType.DMA],
        ),
        cost_estimate=pl.CostEstimate(flops=0, bytes_accessed=4 * count * nel * norb, transcendentals=0),
        name="select",
    )(which, slot, keep, *sources)


def on_device(walkers, propagator, chol, parent_group, parent_slot, live_count):
    slots, nel, norb = walkers.shape
    n_groups, n_vec = lax.axis_size("walker"), lax.axis_size("vec")
    group, plane = lax.axis_index("walker"), lax.axis_index("vec") // CORES
    planes, share = n_vec // CORES, chol.shape[0] // n_groups

    own = lax.dynamic_slice_in_dim(chol, group * share, share, 0)
    near = swap(own, "vec", 1)
    vectors = {0: (own, near)}
    direct = {0: own}

    def send(value, mask, chosen):
        pairs = [(CORES * (p ^ mask) + c, CORES * p + c) for p in range(planes) if chosen(p) for c in range(CORES)]
        return lax.ppermute(value, "vec", pairs)

    for mask in range(1, planes):
        low = mask & -mask
        if low == mask:
            direct[mask] = send(own, mask, lambda p: True)
        else:
            inner = lambda p, mask=mask: abs(p - (p ^ mask)) == 1
            straight = send(own, mask, inner)
            relayed = send(direct[mask ^ low], low, lambda p: not inner(p))
            is_inner = jnp.array([inner(p) for p in range(planes)])[plane]
            direct[mask] = jnp.where(is_inner, straight, relayed)
        vectors[mask] = (direct[mask], swap(direct[mask], "vec", 1))

    moved = jnp.dot(walkers.reshape(slots * nel, norb), propagator, preferred_element_type=jnp.float32)
    moved = moved.astype(jnp.bfloat16).reshape(slots, nel, norb)

    bits = [1 << i for i in range((n_groups - 1).bit_length())]
    half = slots // 2
    pieces = [moved[:half], moved[half:]]
    orders = [bits, bits[1:] + bits[:1]]
    have = [{0: piece} for piece in pieces]
    for step in range(len(bits)):
        for piece in range(2):
            bit = orders[piece][step]
            for mask in list(have[piece]):
                have[piece][mask ^ bit] = swap(have[piece][mask], "walker", bit)

    flat_vectors = [v for mask in range(planes) for v in vectors[mask]]
    blocks = [moved] + [have[piece][mask] for mask in range(1, n_groups) for piece in range(2)]
    terms = energy_terms(blocks, flat_vectors)[:, 0].reshape(n_groups, slots)

    places = ((parent_group[:, 0, :] ^ group) * slots + parent_slot[:, 0, :]).reshape(-1)
    parts = terms.reshape(-1)[places].reshape(n_groups, slots)
    for bit in bits:
        parts = parts + swap(parts, "walker", bit)
    mine = lax.dynamic_index_in_dim(parts, group, 0, keepdims=False)
    keep = jnp.arange(slots, dtype=jnp.int32) < live_count.reshape(())
    factor = 0.5 / (chol.shape[0] * n_vec * nel)
    energy = jnp.where(keep, mine * factor, 0.0).reshape(1, 1, slots)

    my_groups = lax.dynamic_index_in_dim(parent_group[:, 0, :], group, 0, keepdims=False)
    my_slots = lax.dynamic_index_in_dim(parent_slot[:, 0, :], group, 0, keepdims=False)
    which = (my_groups ^ group) * 2 + my_slots // half
    sources = [have[piece][mask] for mask in range(n_groups) for piece in range(2)]
    fresh = select(sources, which, my_slots % half, keep.astype(jnp.int32))
    return fresh, energy


def solution(mesh):
    in_specs = (
        P(("walker", "vec"), None, None),
        P(),
        P("vec", None, None),
        P(None, "vec", None),
        P(None, "vec", None),
        P("walker", "vec"),
    )
    out_specs = (P(("walker", "vec"), None, None), P("walker", "vec", None))
    return jax.shard_map(on_device, mesh=mesh, in_specs=in_specs, out_specs=out_specs, check_vma=False)
```
